32 devices in a mesh: seq: 32 (over z, y, x, core), ch: 1.
Axes of the slice: x: 2, y: 2, z: 4, core: 2. Of those that a mesh axis runs over, the one named last changes fastest.
Arguments:
- q_feat: bfloat16 [8192, 4096], P('seq', 'ch'), may hold values from -6 to 6
- k_feat: bfloat16 [8192, 4096], P('seq', 'ch'), may hold values from -6 to 6
- v_feat: bfloat16 [8192, 4096], P('seq', 'ch'), may hold values from -6 to 6
- short_taps: float32 [3, 3, 4096], P(None, None, 'ch'), may hold values from -3.5 to 3.5
- decay_rate: float32 [16, 4096], P(None, 'ch'), may hold values from 0 to 1, as said below
- residue: float32 [16, 4096], P(None, 'ch'), may hold values from -1 to 1
- skip_gain: float32 [4096], P('ch'), may hold values from -6 to 6
- out_weight: bfloat16 [4096, 4096], P('seq', 'ch'), may hold values from -0.09375 to 0.09375
- doc_starts: int32 [32, 4], P('seq'), may hold values from 0 to 256, as said below
- reset_flags: int32 [32, 4], P('seq'), may hold values from 0 to 1, as said below
Outputs:
- mixer_out: bfloat16 [8192, 4096], P('seq', 'ch')
The draws below stay inside these ranges and needn't reach their ends.
Inputs may be any that keep to these rules, and one draw needn't show every extreme that they name: `doc_starts`: row s lists ascending the offsets within shard s at which documents begin, then unused slots holding 256; a shard holds at most 4 starts, some shard exactly 4, some shard none. `reset_flags`: only used slots hold 1; in each shard at most one slot holds 1, and some shard has one. `decay_rate`: positive rates.
All inputs are finite; a program needn't handle non-finite values.
Results may differ from the reference program's by a relative error of at most 0.018.
Values may be sent and summed in bfloat16 or wider, within the bound.
A program may use at most 256 MiB of HBM per device.

```python
import jax
import jax.numpy as jnp
from jax import lax

D = 4096
MODES = 16
SHORT = 3
BLOCK = 128
SLOTS = 4
TOK = 256
SHARDS = 32
SEQLEN = 8192
GROUP = 4096
N_CH = 1


def rate_table(key):
    picker = jax.random.uniform(jax.random.fold_in(key, 11), (MODES, D))
    fast_rate = jnp.exp(jax.random.uniform(jax.random.fold_in(key, 12), (MODES, D), minval=jnp.log(1.0 / 50.0), maxval=jnp.log(1.0 / 30.0)))
    middle_rate = jnp.exp(jax.random.uniform(jax.random.fold_in(key, 14), (MODES, D), minval=jnp.log(0.25), maxval=jnp.log(2.5))) / TOK
    slow_rate = jnp.exp(jax.random.uniform(jax.random.fold_in(key, 13), (MODES, D), minval=jnp.log(0.1), maxval=jnp.log(2.0))) / SEQLEN
    fast_share = 0.3
    middle_share = 0.3
    chosen = jnp.where(picker < fast_share, fast_rate, jnp.where(picker < fast_share + middle_share, middle_rate, slow_rate))
    return chosen.astype(jnp.float32)


def draw_decay_rate(key, part):
    return rate_table(key)


def draw_residue(key, part):
    rates = rate_table(key)
    base = jnp.clip(jax.random.normal(jax.random.fold_in(key, 22), (MODES, D)), -4.0, 4.0)
    return (0.35 * base * jnp.sqrt(-jnp.expm1(-2.0 * rates))).astype(jnp.float32)


def shard_layout(key):
    base = jax.random.fold_in(key, 7)
    shard_ids = jnp.arange(SHARDS, dtype=jnp.int32)
    full_shard = jax.random.randint(jax.random.fold_in(base, 1), (), 0, SHARDS)
    counts = jax.random.randint(jax.random.fold_in(base, 2), (SHARDS,), 0, SLOTS + 1)
    counts = jnp.where(shard_ids == full_shard, SLOTS, counts)
    counts = jnp.where(shard_ids == (full_shard + 1) % SHARDS, 0, counts)
    scores = jax.random.randint(jax.random.fold_in(base, 3), (SHARDS, TOK), 0, 65536) * TOK + jnp.arange(TOK, dtype=jnp.int32)[None, :]
    _, chosen = lax.top_k(scores, SLOTS)
    chosen = jnp.sort(chosen, axis=1)
    slot_ids = jnp.arange(SLOTS, dtype=jnp.int32)[None, :]
    used_slot = slot_ids < counts[:, None]
    starts = jnp.where(used_slot, chosen, TOK).astype(jnp.int32)
    picked = jax.random.randint(jax.random.fold_in(base, 4), (SHARDS,), 0, 65536) % jnp.maximum(counts, 1)
    coins = (jax.random.randint(jax.random.fold_in(base, 5), (SHARDS,), 0, 16) == 0) | (shard_ids == full_shard)
    flags = ((slot_ids == picked[:, None]) & used_slot & coins[:, None]).astype(jnp.int32)
    return (starts, flags)


def draw_doc_starts(key, part):
    return shard_layout(key)[0]


def draw_reset_flags(key, part):
    return shard_layout(key)[1]


def shard_levels(stream_key, dims, split, least, largest):
    level = 1.0
    for axis_at, shards_of in split:
        steps = jax.random.uniform(jax.random.fold_in(jax.random.fold_in(stream_key, 6), axis_at), (shards_of,), jnp.float32, least / len(split), largest / len(split))
        level = level * jnp.repeat(jnp.exp(steps), dims[axis_at] // shards_of).reshape((-1,) + (1,) * (len(dims) - 1 - axis_at))
    return level


def gaussian(stream_key, dims, width, limit, split=(), kind=jnp.bfloat16):
    gain = shard_levels(stream_key, dims, split, -0.22, 0.18) if split else 1.0
    array = jax.random.normal(stream_key, dims, jnp.float32) * width * gain
    return jnp.minimum(jnp.maximum(array, -limit), limit).astype(kind)


def setup_inputs(seed: int = 0) -> dict:
    key_of = jax.random.split(jax.random.key(seed), 11)
    return {
        "q_feat": gaussian(key_of[0], (SEQLEN, D), 1.0, 6.0, ((0, 32),)),
        "k_feat": gaussian(key_of[1], (SEQLEN, D), 1.0, 6.0, ((0, 32),)),
        "v_feat": gaussian(key_of[2], (SEQLEN, D), 1.0, 6.0, ((0, 32),)),
        "short_taps": gaussian(key_of[3], (3, SHORT, D), 0.6, 3.5, (), jnp.float32),
        "decay_rate": draw_decay_rate(jax.random.fold_in(key_of[10], 71), 0),
        "residue": draw_residue(jax.random.fold_in(key_of[10], 71), 0),
        "skip_gain": gaussian(key_of[6], (D,), 1.0, 6.0, (), jnp.float32),
        "out_weight": gaussian(key_of[7], (D, D), D ** -0.5, 0.09375, ((0, 32),)),
        "doc_starts": draw_doc_starts(jax.random.fold_in(key_of[10], 71), 0),
        "reset_flags": draw_reset_flags(jax.random.fold_in(key_of[10], 71), 0),
    }


def short_filter(features, rim_rows, tap_weights, keep_mask):
    token_rows = features.shape[0]
    tap_count = tap_weights.shape[0]
    joined = jnp.concatenate([rim_rows, features], axis=0)
    summed = tap_weights[0] * features.astype(jnp.float32)
    valid_mask = jnp.ones((token_rows,), jnp.float32)
    for offset in range(1, tap_count):
        valid_mask = valid_mask * jnp.concatenate([jnp.ones((offset - 1,), jnp.float32), keep_mask[:token_rows - offset + 1]])
        lagged = joined[tap_count - 1 - offset:tap_count - 1 - offset + token_rows].astype(jnp.float32)
        summed = summed + tap_weights[offset] * valid_mask[:, None] * lagged
    return summed.astype(jnp.bfloat16)


def document_marks(doc_starts, reset_flags):
    shard_base = (jnp.arange(SHARDS, dtype=jnp.int32) * TOK)[:, None]
    used_slot = doc_starts < TOK
    spots = jnp.where(used_slot, shard_base + doc_starts, SEQLEN).reshape(-1).astype(jnp.int32)
    flagged = ((reset_flags == 1) & used_slot).astype(jnp.float32).reshape(-1)
    starts_at = jnp.zeros((SEQLEN + 1,), jnp.float32).at[spots].max(jnp.ones_like(flagged))[:SEQLEN]
    resets = jnp.zeros((SEQLEN + 1,), jnp.float32).at[spots].max(flagged)[:SEQLEN]
    return starts_at, resets


def modal_filter(gated, resets, decay_rate, residue):
    highest = lax.Precision.HIGHEST
    decay_factor = jnp.exp(-decay_rate)
    steps_axis = jnp.arange(1, BLOCK + 1, dtype=jnp.float32)
    weighted = jnp.exp(-steps_axis[:, None, None] * decay_rate[None]) * residue[None]
    block_pow = jnp.exp(-BLOCK * decay_rate)
    gated_blocks = gated.reshape(SEQLEN // BLOCK, BLOCK, D)
    reset_blocks = resets.reshape(SEQLEN // BLOCK, BLOCK)

    def row_step(carried_state, row_item):
        gated_row, reset_row = row_item
        carried_state = decay_factor * carried_state * (1.0 - reset_row) + gated_row[None, :]
        return carried_state, jnp.sum(residue * carried_state, axis=0)

    def block_step(carried_state, block_item):
        gated_block, reset_block = block_item
        local_end, local_out = lax.scan(row_step, jnp.zeros((MODES, D), jnp.float32), (gated_block, reset_block))
        alive_mask = jnp.cumprod(1.0 - reset_block)
        carried = jnp.einsum("bnc,nc->bc", weighted, carried_state, precision=highest) * alive_mask[:, None]
        next_state = local_end + block_pow * carried_state * alive_mask[-1]
        return next_state, local_out + carried

    _, outputs = lax.scan(block_step, jnp.zeros((MODES, D), jnp.float32), (gated_blocks, reset_blocks))
    return outputs.reshape(SEQLEN, D)


def reference(q_feat, k_feat, v_feat, short_taps, decay_rate, residue, skip_gain, out_weight, doc_starts, reset_flags):
    starts_at, resets = document_marks(doc_starts, reset_flags)
    keep_mask = 1.0 - starts_at
    empty_rim = jnp.zeros((SHORT - 1, D), jnp.bfloat16)
    q_short = short_filter(q_feat, empty_rim, short_taps[0], keep_mask)
    k_short = short_filter(k_feat, empty_rim, short_taps[1], keep_mask)
    v_short = short_filter(v_feat, empty_rim, short_taps[2], keep_mask)
    gated = k_short.astype(jnp.float32) * v_short.astype(jnp.float32)
    filtered = modal_filter(gated, resets, decay_rate, residue)
    mixed = (q_short.astype(jnp.float32) * (filtered + skip_gain[None, :] * gated)).astype(jnp.bfloat16)

    def project_rows(row_block):
        summed = jnp.zeros((TOK, D), jnp.float32)
        for group_index in range(N_CH):
            first = group_index * GROUP
            group_term = jnp.dot(row_block[:, first:first + GROUP], out_weight[:, first:first + GROUP].T, preferred_element_type=jnp.float32)
            rounded = lax.optimization_barrier(group_term.astype(jnp.bfloat16))
            summed = summed + rounded.astype(jnp.float32)
        return summed.astype(jnp.bfloat16)

    projected = lax.map(project_rows, mixed.reshape(SHARDS, TOK, D))
    return projected.reshape(SEQLEN, D)
```

```python
import functools

import jax
import jax.numpy as jnp
from jax import lax
from jax.experimental import pallas as pl
from jax.experimental.pallas import tpu as pltpu
from jax.sharding import PartitionSpec as P

LANES = 128
GROUPS = 8
TILE = LANES * GROUPS
ROWS = 16
UNROLL = 8


def cut_of(starts, flags, tokens):
    cut = jnp.int32(tokens)
    for slot in range(starts.shape[1]):
        cut = jnp.where(flags[0, slot] == 1, jnp.minimum(cut, starts[0, slot]), cut)
    return cut


def local_kernel(starts, flags, q_ref, k_ref, v_ref, rim_ref, taps_ref, rate_ref, res_ref,
                 skip_ref, qs_ref, z_ref, state_ref, fac_ref):
    tokens = q_ref.shape[0]
    modes = rate_ref.shape[0]
    slots = starts.shape[1]
    cut = cut_of(starts, flags, tokens)

    def short_rows(step, carry):
        row = pl.multiple_of(step * ROWS, ROWS)
        back = pl.multiple_of(jnp.maximum(row - ROWS, 0), ROWS)
        at = lax.broadcasted_iota(jnp.int32, (ROWS, LANES), 0) + row
        hit = jnp.zeros((ROWS, LANES), jnp.bool_)
        hit_before = jnp.zeros((ROWS, LANES), jnp.bool_)
        for slot in range(slots):
            hit = hit | (at == starts[0, slot])
            hit_before = hit_before | (at - 1 == starts[0, slot])
        mask1 = jnp.where(hit, 0.0, 1.0)
        mask2 = jnp.where(hit | hit_before, 0.0, 1.0)
        first = step == 0
        for group in range(GROUPS):
            cols = slice(group * LANES, (group + 1) * LANES)

            def short(ref, index):
                x = ref[pl.ds(row, ROWS), cols].astype(jnp.float32)
                before = ref[pl.ds(back, ROWS), cols].astype(jnp.float32)
                rim = rim_ref[index, :, cols].astype(jnp.float32)
                before = jnp.where(first, rim, before)
                both = jnp.concatenate([before, x], axis=0)
                lag1 = pltpu.roll(both, 1, 0)[ROWS:]
                lag2 = pltpu.roll(both, 2, 0)[ROWS:]
                base = 3 * index
                summed = taps_ref[base : base + 1, cols] * x
                summed = summed + taps_ref[base + 1 : base + 2, cols] * mask1 * lag1
                summed = summed + taps_ref[base + 2 : base + 3, cols] * mask2 * lag2
                return summed.astype(jnp.bfloat16)

            qs_ref[pl.ds(row, ROWS), cols] = short(q_ref, 0)
            gated = short(k_ref, 1).astype(jnp.float32) * short(v_ref, 2).astype(jnp.float32)
            z_ref[pl.ds(row * GROUPS + group, ROWS, stride=GROUPS), :] = gated
        return carry

    lax.fori_loop(0, tokens // ROWS, short_rows, 0)

    fac_ref[...] = jnp.exp(-rate_ref[...])
    skip = skip_ref[...]

    def advance(step, states):
        states = list(states)
        for inner in range(UNROLL):
            time = step * UNROLL + inner
            spot = pl.ds(pl.multiple_of(time * GROUPS, GROUPS), GROUPS)
            keep = jnp.where(time == cut, 0.0, 1.0)
            x = z_ref[spot, :]
            sums = [skip * x, None]
            for n in range(modes):
                states[n] = (fac_ref[n] * keep) * states[n] + x
                term = res_ref[n] * states[n]
                sums[n % 2] = term if sums[n % 2] is None else sums[n % 2] + term
            z_ref[spot, :] = sums[0] + sums[1]
        return tuple(states)

    zero = jnp.zeros((GROUPS, LANES), jnp.float32)
    states = lax.fori_loop(0, tokens // UNROLL, advance, (zero,) * modes)
    for n in range(modes):
        state_ref[n] = states[n]
    through = jnp.where(cut < tokens, 0.0, 1.0)
    for n in range(modes, state_ref.shape[0]):
        state_ref[n] = zero + through


def scan_kernel(tokens, pieces_ref, rate_ref, out_ref):
    modes = rate_ref.shape[0]
    factor = jnp.exp(-float(tokens) * rate_ref[...])

    def hop(j, running):
        out_ref[j] = running
        piece = pieces_ref[j]
        return factor * piece[modes : modes + 1] * running + piece[:modes]

    lax.fori_loop(0, pieces_ref.shape[0], hop, jnp.zeros(rate_ref.shape, jnp.float32))


def finish_kernel(starts, flags, qs_ref, z_ref, enter_ref, rate_ref, res_ref, out_ref, fac_ref,
                  y_ref):
    tokens = qs_ref.shape[0]
    modes = rate_ref.shape[0]
    cut = cut_of(starts, flags, tokens)
    fac_ref[...] = jnp.exp(-rate_ref[...])

    def advance(step, weights):
        weights = list(weights)
        for inner in range(UNROLL):
            time = step * UNROLL + inner
            spot = pl.ds(pl.multiple_of(time * GROUPS, GROUPS), GROUPS)
            alive = jnp.where(time < cut, 1.0, 0.0)
            sums = [None, None]
            for n in range(modes):
                sums[n % 2] = weights[n] if sums[n % 2] is None else sums[n % 2] + weights[n]
                weights[n] = weights[n] * fac_ref[n]
            y_ref[spot, :] = z_ref[spot, :] + alive * (sums[0] + sums[1])
        return tuple(weights)

    begin = tuple(res_ref[n] * (fac_ref[n] * enter_ref[n]) for n in range(modes))
    lax.fori_loop(0, tokens // UNROLL, advance, begin)

    def mix_rows(step, carry):
        row = pl.multiple_of(step * ROWS, ROWS)
        for group in range(GROUPS):
            cols = slice(group * LANES, (group + 1) * LANES)
            y = y_ref[pl.ds(row * GROUPS + group, ROWS, stride=GROUPS), :]
            q = qs_ref[pl.ds(row, ROWS), cols].astype(jnp.float32)
            out_ref[pl.ds(row, ROWS), cols] = (q * y).astype(jnp.bfloat16)
        return carry

    lax.fori_loop(0, tokens // ROWS, mix_rows, 0)


def local(q_feat, k_feat, v_feat, short_taps, decay_rate, residue, skip_gain, out_weight,
          doc_starts, reset_flags):
    tokens, channels = q_feat.shape
    modes = decay_rate.shape[0]
    kinds, taps = short_taps.shape[:2]
    n = lax.axis_size("seq")
    me = lax.axis_index("seq")
    tiles = channels // TILE
    heads = modes + 8

    weight = lax.all_gather(out_weight, "seq", axis=0, tiled=True)

    last_is_start = jnp.any(doc_starts[0] == tokens - 1)
    scale = jnp.stack([jnp.where(last_is_start, 0.0, 1.0), jnp.float32(1.0)]).astype(jnp.bfloat16)
    tails = jnp.stack([x[tokens - (taps - 1) :] for x in (q_feat, k_feat, v_feat)])
    tails = tails * scale[None, :, None]
    arrived = lax.ppermute(tails, "seq", [(i, i + 1) for i in range(n - 1)])
    rim = jnp.pad(arrived, ((0, 0), (ROWS - (taps - 1), 0), (0, 0)))

    rates = decay_rate.reshape(modes, channels // LANES, LANES)
    residues = residue.reshape(modes, channels // LANES, LANES)
    skips = skip_gain.reshape(channels // LANES, LANES)

    smem = pl.BlockSpec(memory_space=pltpu.SMEM)
    wide = pl.BlockSpec((tokens, TILE), lambda i: (0, i))
    deep = pl.BlockSpec((modes, GROUPS, LANES), lambda i: (0, i, 0))
    flat = pl.BlockSpec((None, tokens * GROUPS, LANES), lambda i: (i, 0, 0))
    f32 = jnp.float32
    qs, z, state = pl.pallas_call(
        local_kernel,
        grid=(tiles,),
        in_specs=[
            smem, smem, wide, wide, wide,
            pl.BlockSpec((kinds, ROWS, TILE), lambda i: (0, 0, i)),
            pl.BlockSpec((kinds * taps, TILE), lambda i: (0, i)),
            deep, deep,
            pl.BlockSpec((GROUPS, LANES), lambda i: (i, 0)),
        ],
        out_specs=[wide, flat, pl.BlockSpec((heads, GROUPS, LANES), lambda i: (0, i, 0))],
        out_shape=[
            jax.ShapeDtypeStruct((tokens, channels), jnp.bfloat16),
            jax.ShapeDtypeStruct((tiles, tokens * GROUPS, LANES), f32),
            jax.ShapeDtypeStruct((heads, channels // LANES, LANES), f32),
        ],
        scratch_shapes=[pltpu.VMEM((modes, GROUPS, LANES), f32)],
        cost_estimate=pl.CostEstimate(
            flops=tokens * channels * 80, bytes_accessed=tokens * channels * 12, transcendentals=0
        ),
        name="local_filter",
    )(doc_starts, reset_flags, q_feat, k_feat, v_feat, rim,
      short_taps.reshape(kinds * taps, channels), rates, residues, skips)

    part = channels // n
    sent = state.reshape(heads, n, part).transpose(1, 0, 2)
    pieces = lax.all_to_all(sent, "seq", 0, 0)
    my_rates = lax.dynamic_slice_in_dim(decay_rate, me * part, part, 1)
    chained = pl.pallas_call(
        functools.partial(scan_kernel, tokens),
        out_shape=jax.ShapeDtypeStruct((n, modes, part), f32),
        name="chain_states",
    )(pieces, my_rates)
    entering = lax.all_to_all(chained, "seq", 0, 0)
    entering = entering.transpose(1, 0, 2).reshape(modes, channels // LANES, LANES)

    mixed = pl.pallas_call(
        finish_kernel,
        grid=(tiles,),
        in_specs=[smem, smem, wide, flat, deep, deep, deep],
        out_specs=wide,
        out_shape=jax.ShapeDtypeStruct((tokens, channels), jnp.bfloat16),
        scratch_shapes=[
            pltpu.VMEM((modes, GROUPS, LANES), f32),
            pltpu.VMEM((tokens * GROUPS, LANES), f32),
        ],
        cost_estimate=pl.CostEstimate(
            flops=tokens * channels * 40, bytes_accessed=tokens * channels * 8, transcendentals=0
        ),
        name="finish_filter",
    )(doc_starts, reset_flags, qs, z, entering, rates, residues)

    projected = lax.dot_general(
        mixed, weight, (((1,), (1,)), ((), ())), preferred_element_type=f32
    ).astype(jnp.bfloat16)
    return lax.psum_scatter(projected, "ch", scatter_dimension=1, tiled=True)


def solution(mesh):
    placed = (
        P("seq", "ch"), P("seq", "ch"), P("seq", "ch"), P(None, None, "ch"), P(None, "ch"),
        P(None, "ch"), P("ch"), P("seq", "ch"), P("seq", None), P("seq", None),
    )
    return jax.shard_map(
        local, mesh=mesh, in_specs=placed, out_specs=P("seq", "ch"), check_vma=False
    )
```

```python
import functools

import jax
import jax.numpy as jnp
from jax import lax
from jax.experimental import pallas as pl
from jax.experimental.pallas import tpu as pltpu
from jax.sharding import PartitionSpec as P

LANES = 128
GROUPS = 8
TILE = LANES * GROUPS
ROWS = 16
UNROLL = 8
SHARE = 8


def cut_of(starts, flags, tokens):
    cut = jnp.int32(tokens)
    for slot in range(starts.shape[1]):
        cut = jnp.where(flags[0, slot] == 1, jnp.minimum(cut, starts[0, slot]), cut)
    return cut


def local_kernel(starts, flags, q_ref, k_ref, v_ref, rim_ref, taps_ref, rate_ref, res_ref,
                 skip_ref, qs_ref, z_ref, state_ref, fac_ref):
    tokens = q_ref.shape[0]
    modes = rate_ref.shape[0]
    slots = starts.shape[1]
    cut = cut_of(starts, flags, tokens)

    def short_rows(step, carry):
        row = pl.multiple_of(step * ROWS, ROWS)
        back = pl.multiple_of(jnp.maximum(row - ROWS, 0), ROWS)
        at = lax.broadcasted_iota(jnp.int32, (ROWS, LANES), 0) + row
        hit = jnp.zeros((ROWS, LANES), jnp.bool_)
        hit_before = jnp.zeros((ROWS, LANES), jnp.bool_)
        for slot in range(slots):
            hit = hit | (at == starts[0, slot])
            hit_before = hit_before | (at - 1 == starts[0, slot])
        mask1 = jnp.where(hit, 0.0, 1.0)
        mask2 = jnp.where(hit | hit_before, 0.0, 1.0)
        first = step == 0
        for group in range(GROUPS):
            cols = slice(group * LANES, (group + 1) * LANES)

            def short(ref, index):
                x = ref[pl.ds(row, ROWS), cols].astype(jnp.float32)
                before = ref[pl.ds(back, ROWS), cols].astype(jnp.float32)
                rim = rim_ref[index, :, cols].astype(jnp.float32)
                before = jnp.where(first, rim, before)
                both = jnp.concatenate([before, x], axis=0)
                lag1 = pltpu.roll(both, 1, 0)[ROWS:]
                lag2 = pltpu.roll(both, 2, 0)[ROWS:]
                base = 3 * index
                summed = taps_ref[base : base + 1, cols] * x
                summed = summed + taps_ref[base + 1 : base + 2, cols] * mask1 * lag1
                summed = summed + taps_ref[base + 2 : base + 3, cols] * mask2 * lag2
                return summed.astype(jnp.bfloat16)

            qs_ref[pl.ds(row, ROWS), cols] = short(q_ref, 0)
            gated = short(k_ref, 1).astype(jnp.float32) * short(v_ref, 2).astype(jnp.float32)
            z_ref[pl.ds(row * GROUPS + group, ROWS, stride=GROUPS), :] = gated
        return carry

    lax.fori_loop(0, tokens // ROWS, short_rows, 0)

    fac_ref[...] = jnp.exp(-rate_ref[...])
    skip = skip_ref[...]

    def advance(step, states):
        states = list(states)
        for inner in range(UNROLL):
            time = step * UNROLL + inner
            spot = pl.ds(pl.multiple_of(time * GROUPS, GROUPS), GROUPS)
            keep = jnp.where(time == cut, 0.0, 1.0)
            x = z_ref[spot, :]
            sums = [skip * x, None]
            for n in range(modes):
                states[n] = (fac_ref[n] * keep) * states[n] + x
                term = res_ref[n] * states[n]
                sums[n % 2] = term if sums[n % 2] is None else sums[n % 2] + term
            z_ref[spot, :] = sums[0] + sums[1]
        return tuple(states)

    zero = jnp.zeros((GROUPS, LANES), jnp.float32)
    states = lax.fori_loop(0, tokens // UNROLL, advance, (zero,) * modes)
    for n in range(modes):
        state_ref[n] = states[n]
    through = jnp.where(cut < tokens, 0.0, 1.0)
    for n in range(modes, state_ref.shape[0]):
        state_ref[n] = zero + through


def scan_kernel(tokens, pieces_ref, rate_ref, out_ref):
    modes = rate_ref.shape[0]
    factor = jnp.exp(-float(tokens) * rate_ref[...])

    def hop(j, running):
        out_ref[j] = running
        piece = pieces_ref[j]
        return factor * piece[modes : modes + 1] * running + piece[:modes]

    lax.fori_loop(0, pieces_ref.shape[0], hop, jnp.zeros(rate_ref.shape, jnp.float32))


def finish_kernel(starts, flags, qs_ref, z_ref, enter_ref, rate_ref, res_ref, out_ref, fac_ref,
                  y_ref):
    tokens = qs_ref.shape[0]
    modes = rate_ref.shape[0]
    cut = cut_of(starts, flags, tokens)
    fac_ref[...] = jnp.exp(-rate_ref[...])

    def advance(step, weights):
        weights = list(weights)
        for inner in range(UNROLL):
            time = step * UNROLL + inner
            spot = pl.ds(pl.multiple_of(time * GROUPS, GROUPS), GROUPS)
            alive = jnp.where(time < cut, 1.0, 0.0)
            sums = [None, None]
            for n in range(modes):
                sums[n % 2] = weights[n] if sums[n % 2] is None else sums[n % 2] + weights[n]
                weights[n] = weights[n] * fac_ref[n]
            y_ref[spot, :] = z_ref[spot, :] + alive * (sums[0] + sums[1])
        return tuple(weights)

    begin = tuple(res_ref[n] * (fac_ref[n] * enter_ref[n]) for n in range(modes))
    lax.fori_loop(0, tokens // UNROLL, advance, begin)

    def mix_rows(step, carry):
        row = pl.multiple_of(step * ROWS, ROWS)
        for group in range(GROUPS):
            cols = slice(group * LANES, (group + 1) * LANES)
            y = y_ref[pl.ds(row * GROUPS + group, ROWS, stride=GROUPS), :]
            q = qs_ref[pl.ds(row, ROWS), cols].astype(jnp.float32)
            out_ref[pl.ds(row, ROWS), cols] = (q * y).astype(jnp.bfloat16)
        return carry

    lax.fori_loop(0, tokens // ROWS, mix_rows, 0)


def doubling(block, order, n):
    me = lax.axis_index("seq")
    held = block[None]
    for bit in order:
        other = lax.ppermute(held, "seq", [(i, i ^ (1 << bit)) for i in range(n)])
        upper = lax.rem(lax.div(me, 1 << bit), 2) == 1
        held = jnp.where(
            upper, jnp.concatenate([other, held]), jnp.concatenate([held, other])
        )
    return held


def local(q_feat, k_feat, v_feat, short_taps, decay_rate, residue, skip_gain, out_weight,
          doc_starts, reset_flags):
    tokens, channels = q_feat.shape
    modes = decay_rate.shape[0]
    kinds, taps = short_taps.shape[:2]
    n = lax.axis_size("seq")
    me = lax.axis_index("seq")
    tiles = channels // TILE
    heads = modes + 8

    bits = n.bit_length() - 1
    share = channels // SHARE if n == 1 << bits and bits >= 3 else 0
    high = tuple(range(bits - 1, 2, -1))
    orders = (high + (1, 2, 0), high + (2, 1, 0))
    doubled = [
        doubling(out_weight[:, i * share : (i + 1) * share], order, n)
        for i, order in enumerate(orders)
        if share
    ]
    weight = lax.all_gather(out_weight[:, 2 * share :], "seq", axis=0, tiled=True)

    last_is_start = jnp.any(doc_starts[0] == tokens - 1)
    scale = jnp.stack([jnp.where(last_is_start, 0.0, 1.0), jnp.float32(1.0)]).astype(jnp.bfloat16)
    tails = jnp.stack([x[tokens - (taps - 1) :] for x in (q_feat, k_feat, v_feat)])
    tails = tails * scale[None, :, None]
    arrived = lax.ppermute(tails, "seq", [(i, i + 1) for i in range(n - 1)])
    rim = jnp.pad(arrived, ((0, 0), (ROWS - (taps - 1), 0), (0, 0)))

    rates = decay_rate.reshape(modes, channels // LANES, LANES)
    residues = residue.reshape(modes, channels // LANES, LANES)
    skips = skip_gain.reshape(channels // LANES, LANES)

    smem = pl.BlockSpec(memory_space=pltpu.SMEM)
    wide = pl.BlockSpec((tokens, TILE), lambda i: (0, i))
    deep = pl.BlockSpec((modes, GROUPS, LANES), lambda i: (0, i, 0))
    flat = pl.BlockSpec((None, tokens * GROUPS, LANES), lambda i: (i, 0, 0))
    f32 = jnp.float32
    qs, z, state = pl.pallas_call(
        local_kernel,
        grid=(tiles,),
        in_specs=[
            smem, smem, wide, wide, wide,
            pl.BlockSpec((kinds, ROWS, TILE), lambda i: (0, 0, i)),
            pl.BlockSpec((kinds * taps, TILE), lambda i: (0, i)),
            deep, deep,
            pl.BlockSpec((GROUPS, LANES), lambda i: (i, 0)),
        ],
        out_specs=[wide, flat, pl.BlockSpec((heads, GROUPS, LANES), lambda i: (0, i, 0))],
        out_shape=[
            jax.ShapeDtypeStruct((tokens, channels), jnp.bfloat16),
            jax.ShapeDtypeStruct((tiles, tokens * GROUPS, LANES), f32),
            jax.ShapeDtypeStruct((heads, channels // LANES, LANES), f32),
        ],
        scratch_shapes=[pltpu.VMEM((modes, GROUPS, LANES), f32)],
        cost_estimate=pl.CostEstimate(
            flops=tokens * channels * 80, bytes_accessed=tokens * channels * 12, transcendentals=0
        ),
        name="local_filter",
    )(doc_starts, reset_flags, q_feat, k_feat, v_feat, rim,
      short_taps.reshape(kinds * taps, channels), rates, residues, skips)

    part = channels // n
    sent = state.reshape(heads, n, part).transpose(1, 0, 2)
    pieces = lax.all_to_all(sent, "seq", 0, 0)
    my_rates = lax.dynamic_slice_in_dim(decay_rate, me * part, part, 1)
    chained = pl.pallas_call(
        functools.partial(scan_kernel, tokens),
        out_shape=jax.ShapeDtypeStruct((n, modes, part), f32),
        name="chain_states",
    )(pieces, my_rates)
    entering = lax.all_to_all(chained, "seq", 0, 0)
    entering = entering.transpose(1, 0, 2).reshape(modes, channels // LANES, LANES)

    mixed = pl.pallas_call(
        finish_kernel,
        grid=(tiles,),
        in_specs=[smem, smem, wide, flat, deep, deep, deep],
        out_specs=wide,
        out_shape=jax.ShapeDtypeStruct((tokens, channels), jnp.bfloat16),
        scratch_shapes=[
            pltpu.VMEM((modes, GROUPS, LANES), f32),
            pltpu.VMEM((tokens * GROUPS, LANES), f32),
        ],
        cost_estimate=pl.CostEstimate(
            flops=tokens * channels * 40, bytes_accessed=tokens * channels * 8, transcendentals=0
        ),
        name="finish_filter",
    )(doc_starts, reset_flags, qs, z, entering, rates, residues)

    def project(columns, rows):
        return lax.dot_general(
            columns, rows, (((1,), (1,)), ((), ())), preferred_element_type=f32
        )

    early = jnp.zeros((), f32)
    features = out_weight.shape[0]
    for i, (order, rows) in enumerate(zip(orders, doubled)):
        term = project(mixed[:, i * share : (i + 1) * share], rows.reshape(n * features, share))
        term = term.reshape((tokens,) + (2,) * bits + (features,))
        foremost = order[::-1]
        axes = tuple(1 + foremost.index(bit) for bit in range(bits - 1, -1, -1))
        term = term.transpose((0,) + axes + (bits + 1,)).reshape(tokens, n * features)
        early = early + term
    projected = (project(mixed[:, 2 * share :], weight) + early).astype(jnp.bfloat16)
    return lax.psum_scatter(projected, "ch", scatter_dimension=1, tiled=True)


def solution(mesh):
    placed = (
        P("seq", "ch"), P("seq", "ch"), P("seq", "ch"), P(None, None, "ch"), P(None, "ch"),
        P(None, "ch"), P("ch"), P("seq", "ch"), P("seq", None), P("seq", None),
    )
    return jax.shard_map(
        local, mesh=mesh, in_specs=placed, out_specs=P("seq", "ch"), check_vma=False
    )
```

```python
import functools

import jax
import jax.numpy as jnp
from jax import lax
from jax.experimental import pallas as pl
from jax.experimental.pallas import tpu as pltpu
from jax.sharding import PartitionSpec as P

LANES = 128
GROUPS = 8
TILE = LANES * GROUPS
ROWS = 16
UNROLL = 8
SHARE = 8


def cut_of(starts, flags, tokens):
    cut = jnp.int32(tokens)
    for slot in range(starts.shape[1]):
        cut = jnp.where(flags[0, slot] == 1, jnp.minimum(cut, starts[0, slot]), cut)
    return cut


def local_kernel(starts, flags, q_ref, k_ref, v_ref, rim_ref, taps_ref, rate_ref, res_ref,
                 skip_ref, qs_ref, z_ref, state_ref, fac_ref):
    tokens = q_ref.shape[0]
    modes = rate_ref.shape[0]
    slots = starts.shape[1]
    cut = cut_of(starts, flags, tokens)

    def short_rows(step, carry):
        row = pl.multiple_of(step * ROWS, ROWS)
        back = pl.multiple_of(jnp.maximum(row - ROWS, 0), ROWS)
        at = lax.broadcasted_iota(jnp.int32, (ROWS, LANES), 0) + row
        hit = jnp.zeros((ROWS, LANES), jnp.bool_)
        hit_before = jnp.zeros((ROWS, LANES), jnp.bool_)
        for slot in range(slots):
            hit = hit | (at == starts[0, slot])
            hit_before = hit_before | (at - 1 == starts[0, slot])
        mask1 = jnp.where(hit, 0.0, 1.0)
        mask2 = jnp.where(hit | hit_before, 0.0, 1.0)
        first = step == 0
        for group in range(GROUPS):
            cols = slice(group * LANES, (group + 1) * LANES)

            def short(ref, index):
                x = ref[pl.ds(row, ROWS), cols].astype(jnp.float32)
                before = ref[pl.ds(back, ROWS), cols].astype(jnp.float32)
                rim = rim_ref[index, :, cols].astype(jnp.float32)
                before = jnp.where(first, rim, before)
                both = jnp.concatenate([before, x], axis=0)
                lag1 = pltpu.roll(both, 1, 0)[ROWS:]
                lag2 = pltpu.roll(both, 2, 0)[ROWS:]
                base = 3 * index
                summed = taps_ref[base : base + 1, cols] * x
                summed = summed + taps_ref[base + 1 : base + 2, cols] * mask1 * lag1
                summed = summed + taps_ref[base + 2 : base + 3, cols] * mask2 * lag2
                return summed.astype(jnp.bfloat16)

            qs_ref[pl.ds(row, ROWS), cols] = short(q_ref, 0)
            gated = short(k_ref, 1).astype(jnp.float32) * short(v_ref, 2).astype(jnp.float32)
            z_ref[pl.ds(row * GROUPS + group, ROWS, stride=GROUPS), :] = gated
        return carry

    lax.fori_loop(0, tokens // ROWS, short_rows, 0)

    fac_ref[...] = jnp.exp(-rate_ref[...])
    skip = skip_ref[...]

    def advance(step, states):
        states = list(states)
        for inner in range(UNROLL):
            time = step * UNROLL + inner
            spot = pl.ds(pl.multiple_of(time * GROUPS, GROUPS), GROUPS)
            keep = jnp.where(time == cut, 0.0, 1.0)
            x = z_ref[spot, :]
            sums = [skip * x, None]
            for n in range(modes):
                states[n] = (fac_ref[n] * keep) * states[n] + x
                term = res_ref[n] * states[n]
                sums[n % 2] = term if sums[n % 2] is None else sums[n % 2] + term
            z_ref[spot, :] = sums[0] + sums[1]
        return tuple(states)

    zero = jnp.zeros((GROUPS, LANES), jnp.float32)
    states = lax.fori_loop(0, tokens // UNROLL, advance, (zero,) * modes)
    for n in range(modes):
        state_ref[n] = states[n]
    through = jnp.where(cut < tokens, 0.0, 1.0)
    for n in range(modes, state_ref.shape[0]):
        state_ref[n] = zero + through


def scan_kernel(tokens, pieces_ref, rate_ref, out_ref):
    modes = rate_ref.shape[0]
    factor = jnp.exp(-float(tokens) * rate_ref[...])

    def hop(j, running):
        out_ref[j] = running
        piece = pieces_ref[j]
        return factor * piece[modes : modes + 1] * running + piece[:modes]

    lax.fori_loop(0, pieces_ref.shape[0], hop, jnp.zeros(rate_ref.shape, jnp.float32))


def finish_kernel(starts, flags, qs_ref, z_ref, enter_ref, rate_ref, res_ref, out_ref, fac_ref,
                  y_ref):
    tokens = qs_ref.shape[0]
    modes = rate_ref.shape[0]
    cut = cut_of(starts, flags, tokens)
    fac_ref[...] = jnp.exp(-rate_ref[...])

    def advance(step, weights):
        weights = list(weights)
        for inner in range(UNROLL):
            time = step * UNROLL + inner
            spot = pl.ds(pl.multiple_of(time * GROUPS, GROUPS), GROUPS)
            alive = jnp.where(time < cut, 1.0, 0.0)
            sums = [None, None]
            for n in range(modes):
                sums[n % 2] = weights[n] if sums[n % 2] is None else sums[n % 2] + weights[n]
                weights[n] = weights[n] * fac_ref[n]
            y_ref[spot, :] = z_ref[spot, :] + alive * (sums[0] + sums[1])
        return tuple(weights)

    begin = tuple(res_ref[n] * (fac_ref[n] * enter_ref[n]) for n in range(modes))
    lax.fori_loop(0, tokens // UNROLL, advance, begin)

    def mix_rows(step, carry):
        row = pl.multiple_of(step * ROWS, ROWS)
        for group in range(GROUPS):
            cols = slice(group * LANES, (group + 1) * LANES)
            y = y_ref[pl.ds(row * GROUPS + group, ROWS, stride=GROUPS), :]
            q = qs_ref[pl.ds(row, ROWS), cols].astype(jnp.float32)
            out_ref[pl.ds(row, ROWS), cols] = (q * y).astype(jnp.bfloat16)
        return carry

    lax.fori_loop(0, tokens // ROWS, mix_rows, 0)


def doubling(block, order, n, beside):
    me = lax.axis_index("seq")
    held = block[None]
    for stage, bit in enumerate(order):
        other = lax.ppermute(held, "seq", [(i, i ^ (1 << bit)) for i in range(n)])
        if stage < len(beside):
            other, _ = lax.optimization_barrier((other, beside[stage]))
        upper = lax.rem(lax.div(me, 1 << bit), 2) == 1
        held = jnp.where(
            upper, jnp.concatenate([other, held]), jnp.concatenate([held, other])
        )
    return held


def local(q_feat, k_feat, v_feat, short_taps, decay_rate, residue, skip_gain, out_weight,
          doc_starts, reset_flags):
    tokens, channels = q_feat.shape
    modes = decay_rate.shape[0]
    kinds, taps = short_taps.shape[:2]
    n = lax.axis_size("seq")
    me = lax.axis_index("seq")
    tiles = channels // TILE
    heads = modes + 8

    bits = n.bit_length() - 1
    share = channels // SHARE if n == 1 << bits and bits >= 3 else 0
    high = tuple(range(bits - 1, 2, -1))
    orders = (high + (1, 2, 0), high + (2, 1, 0))
    weight = lax.all_gather(out_weight[:, 2 * share :], "seq", axis=0, tiled=True)

    last_is_start = jnp.any(doc_starts[0] == tokens - 1)
    scale = jnp.stack([jnp.where(last_is_start, 0.0, 1.0), jnp.float32(1.0)]).astype(jnp.bfloat16)
    tails = jnp.stack([x[tokens - (taps - 1) :] for x in (q_feat, k_feat, v_feat)])
    tails = tails * scale[None, :, None]
    arrived = lax.ppermute(tails, "seq", [(i, i + 1) for i in range(n - 1)])
    rim = jnp.pad(arrived, ((0, 0), (ROWS - (taps - 1), 0), (0, 0)))

    rates = decay_rate.reshape(modes, channels // LANES, LANES)
    residues = residue.reshape(modes, channels // LANES, LANES)
    skips = skip_gain.reshape(channels // LANES, LANES)

    smem = pl.BlockSpec(memory_space=pltpu.SMEM)
    wide = pl.BlockSpec((tokens, TILE), lambda i: (0, i))
    deep = pl.BlockSpec((modes, GROUPS, LANES), lambda i: (0, i, 0))
    flat = pl.BlockSpec((None, tokens * GROUPS, LANES), lambda i: (i, 0, 0))
    f32 = jnp.float32
    qs, z, state = pl.pallas_call(
        local_kernel,
        grid=(tiles,),
        in_specs=[
            smem, smem, wide, wide, wide,
            pl.BlockSpec((kinds, ROWS, TILE), lambda i: (0, 0, i)),
            pl.BlockSpec((kinds * taps, TILE), lambda i: (0, i)),
            deep, deep,
            pl.BlockSpec((GROUPS, LANES), lambda i: (i, 0)),
        ],
        out_specs=[wide, flat, pl.BlockSpec((heads, GROUPS, LANES), lambda i: (0, i, 0))],
        out_shape=[
            jax.ShapeDtypeStruct((tokens, channels), jnp.bfloat16),
            jax.ShapeDtypeStruct((tiles, tokens * GROUPS, LANES), f32),
            jax.ShapeDtypeStruct((heads, channels // LANES, LANES), f32),
        ],
        scratch_shapes=[pltpu.VMEM((modes, GROUPS, LANES), f32)],
        cost_estimate=pl.CostEstimate(
            flops=tokens * channels * 80, bytes_accessed=tokens * channels * 12, transcendentals=0
        ),
        name="local_filter",
    )(doc_starts, reset_flags, q_feat, k_feat, v_feat, rim,
      short_taps.reshape(kinds * taps, channels), rates, residues, skips)

    part = channels // n
    sent = state.reshape(heads, n, part).transpose(1, 0, 2)
    pieces = lax.all_to_all(sent, "seq", 0, 0)
    my_rates = lax.dynamic_slice_in_dim(decay_rate, me * part, part, 1)
    chained = pl.pallas_call(
        functools.partial(scan_kernel, tokens),
        out_shape=jax.ShapeDtypeStruct((n, modes, part), f32),
        name="chain_states",
    )(pieces, my_rates)
    entering = lax.all_to_all(chained, "seq", 0, 0)
    entering = entering.transpose(1, 0, 2).reshape(modes, channels // LANES, LANES)

    mixed = pl.pallas_call(
        finish_kernel,
        grid=(tiles,),
        in_specs=[smem, smem, wide, flat, deep, deep, deep],
        out_specs=wide,
        out_shape=jax.ShapeDtypeStruct((tokens, channels), jnp.bfloat16),
        scratch_shapes=[
            pltpu.VMEM((modes, GROUPS, LANES), f32),
            pltpu.VMEM((tokens * GROUPS, LANES), f32),
        ],
        cost_estimate=pl.CostEstimate(
            flops=tokens * channels * 40, bytes_accessed=tokens * channels * 8, transcendentals=0
        ),
        name="finish_filter",
    )(doc_starts, reset_flags, qs, z, entering, rates, residues)

    doubled = [
        doubling(out_weight[:, i * share : (i + 1) * share], order, n, (qs, pieces, entering, mixed))
        for i, order in enumerate(orders)
        if share
    ]

    def project(columns, rows):
        return lax.dot_general(
            columns, rows, (((1,), (1,)), ((), ())), preferred_element_type=f32
        )

    early = jnp.zeros((), f32)
    features = out_weight.shape[0]
    for i, (order, rows) in enumerate(zip(orders, doubled)):
        term = project(mixed[:, i * share : (i + 1) * share], rows.reshape(n * features, share))
        term = term.reshape((tokens,) + (2,) * bits + (features,))
        foremost = order[::-1]
        axes = tuple(1 + foremost.index(bit) for bit in range(bits - 1, -1, -1))
        term = term.transpose((0,) + axes + (bits + 1,)).reshape(tokens, n * features)
        early = early + term
    projected = (project(mixed[:, 2 * share :], weight) + early).astype(jnp.bfloat16)
    return lax.psum_scatter(projected, "ch", scatter_dimension=1, tiled=True)


def solution(mesh):
    placed = (
        P("seq", "ch"), P("seq", "ch"), P("seq", "ch"), P(None, None, "ch"), P(None, "ch"),
        P(None, "ch"), P("ch"), P("seq", "ch"), P("seq", None), P("seq", None),
    )
    return jax.shard_map(
        local, mesh=mesh, in_specs=placed, out_specs=P("seq", "ch"), check_vma=False
    )
```
